32 devices in a mesh: grp: 2 (over x), tm: 16 (over z, y, core).
Axes of the slice: x: 2, y: 2, z: 4, core: 2. Of those that a mesh axis runs over, the one named last changes fastest.
Arguments:
- upsampled: bfloat16 [2, 12288, 512], P(None, ('grp', 'tm')), parts along dimension 1, may hold values from -6 to 6
- taps: bfloat16 [3, 7, 512, 512], replicated, may hold values from -0.09375 to 0.09375
- bias_wide: float32 [3, 512], replicated, may hold values from -1.8 to 1.8
- pointwise: bfloat16 [3, 512, 512], replicated, may hold values from -0.25 to 0.25
- bias_point: float32 [3, 512], replicated, may hold values from -1.8 to 1.8
- alpha_in: float32 [3, 512], replicated, may hold values from 0.5 to 4
- beta_in: float32 [3, 512], replicated, may hold values from 0.5 to 4
- alpha_mid: float32 [3, 512], replicated, may hold values from 0.5 to 4
- beta_mid: float32 [3, 512], replicated, may hold values from 0.5 to 4
Outputs:
- decoded: bfloat16 [12288, 512], P(('grp', 'tm')), parts along dimension 0
The draws below stay inside these ranges and needn't reach their ends.
There are 2 independent parts, one for each index of `grp`. The reference program is written for one: setup_inputs(seed, part) draws one part's arguments, and reference() takes and returns one part's arrays. A program takes and returns all parts, laid end to end along the dimension named above; an argument that names none is the same for every part. Nothing has to cross between parts.
All inputs are finite; a program needn't handle non-finite values.
Results may differ from the reference program's by a relative error of at most 0.027.
The reference program's roundings to bfloat16 on the way count: a program that leaves them out, or rounds other values in their place, can miss the bound.
Values may be sent and summed in bfloat16 or wider, within the bound.
A program may use at most 128 MiB of HBM per device.

```python
import math
import jax
import jax.numpy as jnp

C = 512
KERNEL = 7
STRIDE = 8
UNITS = 3
FRAMES = 6144


def block_levels(stream_key, dims, shards, smallest, high):
    def one(position, parts):
        draws = jax.random.uniform(jax.random.fold_in(jax.random.fold_in(stream_key, 6), position), (parts,), jnp.float32, smallest / len(shards), high / len(shards))
        return jnp.repeat(jnp.exp(draws), dims[position] // parts).reshape((-1,) + (1,) * (len(dims) - position - 1))

    gain = one(*shards[0])
    for cut in shards[1:]:
        gain = gain * one(*cut)
    return gain


def noise(own_key, extent, deviation, most, shards=(), kind=jnp.bfloat16):
    loudness = block_levels(own_key, extent, shards, -0.22, 0.18) if shards else 1.0
    array = jax.random.normal(own_key, extent, jnp.float32) * deviation * loudness
    return jnp.minimum(jnp.maximum(array, -most), most).astype(kind)


def setup_inputs(seed: int = 0, part: int = 0) -> dict:
    key_list = jax.random.split(jax.random.key(seed), 10)
    part_keys = jax.random.split(jax.random.fold_in(key_list[9], part), 10)
    return {
        "upsampled": noise(part_keys[0], (2, FRAMES, C), 1.0, 6.0, ((1, 16),)),
        "taps": noise(key_list[1], (UNITS, KERNEL, C, C), (KERNEL * C) ** -0.5, 0.09375),
        "bias_wide": noise(key_list[2], (UNITS, C), 0.3, 1.8, (), jnp.float32),
        "pointwise": noise(key_list[3], (UNITS, C, C), C ** -0.5, 0.25),
        "bias_point": noise(key_list[4], (UNITS, C), 0.3, 1.8, (), jnp.float32),
        "alpha_in": jnp.clip(jnp.exp(jax.random.uniform(key_list[5], (UNITS, C), jnp.float32, math.log(0.5), math.log(4.0))), 0.5, 4.0),
        "beta_in": jnp.clip(jnp.exp(jax.random.uniform(key_list[6], (UNITS, C), jnp.float32, math.log(0.5), math.log(4.0))), 0.5, 4.0),
        "alpha_mid": jnp.clip(jnp.exp(jax.random.uniform(key_list[7], (UNITS, C), jnp.float32, math.log(0.5), math.log(4.0))), 0.5, 4.0),
        "beta_mid": jnp.clip(jnp.exp(jax.random.uniform(key_list[8], (UNITS, C), jnp.float32, math.log(0.5), math.log(4.0))), 0.5, 4.0),
    }


def snake(values, alpha, beta):
    return values + jnp.square(jnp.sin(alpha * values)) / beta


def residual_unit(inputs, dilation, taps, bias_wide, pointwise, bias_point, alpha_in, beta_in, alpha_mid, beta_mid):
    length = inputs.shape[0] - 6 * dilation
    widened = snake(inputs.astype(jnp.float32), alpha_in, beta_in).astype(jnp.bfloat16)
    middle = jnp.zeros((length, taps.shape[2]), jnp.float32) + bias_wide
    for k in range(KERNEL):
        middle = middle + jnp.dot(widened[k * dilation:k * dilation + length], taps[k], preferred_element_type=jnp.float32)
    gated = snake(middle, alpha_mid, beta_mid).astype(jnp.bfloat16)
    update = jnp.dot(gated, pointwise, preferred_element_type=jnp.float32) + bias_point
    kept = inputs[3 * dilation:3 * dilation + length].astype(jnp.float32)
    return (kept + update).astype(jnp.bfloat16)


def reference(upsampled, taps, bias_wide, pointwise, bias_point, alpha_in, beta_in, alpha_mid, beta_mid):
    frames = upsampled.shape[1]
    shifted = jnp.concatenate([jnp.zeros((STRIDE, upsampled.shape[2]), upsampled.dtype), upsampled[1, :frames - STRIDE]], axis=0)
    current = (upsampled[0].astype(jnp.float32) + shifted.astype(jnp.float32)).astype(jnp.bfloat16)
    dilations = (1, 3, 9)
    for index in range(UNITS):
        spread = 3 * dilations[index]
        padded = jnp.pad(current, ((spread, spread), (0, 0)))
        current = residual_unit(padded, dilations[index], taps[index], bias_wide[index], pointwise[index], bias_point[index], alpha_in[index], beta_in[index], alpha_mid[index], beta_mid[index])
    return current
```

```python
import functools
import math

import jax
import jax.numpy as jnp
from jax import lax
from jax.experimental import pallas as pl
from jax.experimental.pallas import tpu as pltpu
from jax.sharding import PartitionSpec as P

KERNEL = 7
STRIDE = 8
UNITS = 3
DILATIONS = (1, 3, 9)
SPREAD = 3 * max(DILATIONS)
REACH = 3 * sum(DILATIONS)
ROWS = 16
EDGE = 48
LEAD = EDGE - STRIDE
SINE = (3.141592640130706, -5.167710083507895, 2.550077523214613, -0.5982912856202587, 0.07765766030474007)


def snake(values, frequency, inverse):
    turns = values * frequency
    rest = turns - jnp.round(turns)
    square = rest * rest
    poly = SINE[-1]
    for coefficient in SINE[-2::-1]:
        poly = poly * square + coefficient
    sine = poly * rest
    return values + sine * sine * inverse


def kernel(
    count, frames, tiles, chunks,
    up_ref, low_ref, high_ref, taps_hbm, point_hbm, bias_wide, bias_point,
    alpha_in, beta_in, alpha_mid, beta_mid,
    out_ref,
    taps_ref, point_ref, ext_ref, x_ref, s_ref, sems,
):
    rows = tiles * ROWS
    extended = frames + 2 * EDGE
    copies = []
    for unit in range(UNITS):
        copies.append((
            pltpu.make_async_copy(taps_hbm.at[unit], taps_ref.at[unit], sems.at[0, unit]),
            pltpu.make_async_copy(point_hbm.at[unit], point_ref.at[unit], sems.at[1, unit]),
        ))
    for pair in copies:
        for copy in pair:
            copy.start()
    me = lax.axis_index("tm")
    for part in range(2):
        base = part * extended
        ext_ref[base : base + EDGE, :] = low_ref[part]
        ext_ref[base + EDGE : base + EDGE + frames, :] = up_ref[part]
        ext_ref[base + EDGE + frames : base + extended, :] = high_ref[part]

    def frame_of(row):
        return (row & (ROWS - 1)) * tiles + (row >> 4)

    row = lax.broadcasted_iota(jnp.int32, (rows, 2 * extended), 0)
    column = lax.broadcasted_iota(jnp.int32, (rows, 2 * extended), 1)
    source = frame_of(row)
    hit = (column == source + STRIDE) | (column == source + extended)
    spread = jnp.where(hit, 1.0, 0.0).astype(jnp.bfloat16)
    x_ref[...] = jnp.dot(spread, ext_ref[...], preferred_element_type=jnp.float32).astype(jnp.bfloat16)

    lane_row = lax.broadcasted_iota(jnp.int32, (ROWS, 128), 0) * tiles
    first = LEAD - me * frames
    last = first + count * frames
    channels = x_ref.shape[1]

    for unit in range(UNITS):
        reach = 3 * DILATIONS[unit]
        frequency = alpha_in[unit : unit + 1, :] * (1.0 / math.pi)
        inverse = 1.0 / beta_in[unit : unit + 1, :]
        for tile in range(tiles):
            v = x_ref[tile * ROWS : (tile + 1) * ROWS, :].astype(jnp.float32)
            s = snake(v, frequency, inverse)
            where = lane_row + tile
            inside = (where >= first) & (where < last)
            s = jnp.concatenate(
                [jnp.where(inside, s[:, c : c + 128], 0.0) for c in range(0, channels, 128)], axis=1
            )
            start = (SPREAD + tile) * ROWS
            s_ref[start : start + ROWS, :] = s.astype(jnp.bfloat16)
            if tile >= tiles - reach:
                start = (SPREAD + tile - tiles) * ROWS
                s_ref[start : start + ROWS, :] = pltpu.roll(s, 1, 0).astype(jnp.bfloat16)
            if tile < reach:
                start = (SPREAD + tile + tiles) * ROWS
                s_ref[start : start + ROWS, :] = pltpu.roll(s, ROWS - 1, 0).astype(jnp.bfloat16)
        frequency = alpha_mid[unit : unit + 1, :] * (1.0 / math.pi)
        inverse = 1.0 / beta_mid[unit : unit + 1, :]
        copies[unit][0].wait()
        copies[unit][1].wait()
        begin = 0
        for size in chunks:
            length = size * ROWS
            stacked = jnp.concatenate(
                [
                    s_ref[pl.ds((SPREAD + begin + (k - 3) * DILATIONS[unit]) * ROWS, length), :]
                    for k in range(KERNEL)
                ],
                axis=1,
            )
            h = jnp.dot(stacked, taps_ref[unit], preferred_element_type=jnp.float32)
            h = h + bias_wide[unit : unit + 1, :]
            g = snake(h, frequency, inverse).astype(jnp.bfloat16)
            update = jnp.dot(g, point_ref[unit], preferred_element_type=jnp.float32)
            span = slice(begin * ROWS, begin * ROWS + length)
            kept = x_ref[span, :].astype(jnp.float32)
            x_ref[span, :] = (kept + (update + bias_point[unit : unit + 1, :])).astype(jnp.bfloat16)
            begin += size

    row = lax.broadcasted_iota(jnp.int32, (frames, rows), 0)
    column = lax.broadcasted_iota(jnp.int32, (frames, rows), 1)
    gather = jnp.where(frame_of(column) == row + LEAD, 1.0, 0.0).astype(jnp.bfloat16)
    out_ref[...] = jnp.dot(gather, x_ref[...], preferred_element_type=jnp.float32).astype(jnp.bfloat16)


def per_device(
    upsampled, taps, bias_wide, pointwise, bias_point, alpha_in, beta_in, alpha_mid, beta_mid
):
    count = lax.axis_size("tm")
    frames, channels = upsampled.shape[1:]
    tiles = -(-(frames + LEAD + REACH) // ROWS)
    rows = tiles * ROWS
    forward = [(i, i + 1) for i in range(count - 1)]
    backward = [(i + 1, i) for i in range(count - 1)]
    low = lax.ppermute(upsampled[:, frames - EDGE :], "tm", forward)
    high = lax.ppermute(upsampled[:, :EDGE], "tm", backward)
    half = (tiles + 1) // 2
    vmem = pl.BlockSpec(memory_space=pltpu.VMEM)
    hbm = pl.BlockSpec(memory_space=pl.ANY)
    return pl.pallas_call(
        functools.partial(kernel, count, frames, tiles, (half, tiles - half)),
        out_shape=jax.ShapeDtypeStruct((frames, channels), jnp.bfloat16),
        in_specs=[vmem, vmem, vmem, hbm, hbm] + [vmem] * 6,
        out_specs=vmem,
        scratch_shapes=[
            pltpu.VMEM((UNITS, KERNEL * channels, channels), jnp.bfloat16),
            pltpu.VMEM((UNITS, channels, channels), jnp.bfloat16),
            pltpu.VMEM((2 * (frames + 2 * EDGE), channels), jnp.bfloat16),
            pltpu.VMEM((rows, channels), jnp.bfloat16),
            pltpu.VMEM((rows + 2 * SPREAD * ROWS, channels), jnp.bfloat16),
            pltpu.SemaphoreType.DMA((2, UNITS)),
        ],
        compiler_params=pltpu.CompilerParams(vmem_limit_bytes=48 << 20),
    )(
        upsampled, low, high, taps.reshape(UNITS, KERNEL * channels, channels), pointwise,
        bias_wide, bias_point, alpha_in, beta_in, alpha_mid, beta_mid,
    )


def solution(mesh):
    placed = (P(None, ("grp", "tm"), None), P(), P(), P(), P(), P(), P(), P(), P())
    return jax.shard_map(
        per_device, mesh=mesh, in_specs=placed, out_specs=P(("grp", "tm"), None), check_vma=False
    )
```

```python
import functools
import math

import jax
import jax.numpy as jnp
from jax import lax
from jax.experimental import pallas as pl
from jax.experimental.pallas import tpu as pltpu
from jax.sharding import PartitionSpec as P

MESH = pl.DeviceIdType.MESH
KERNEL = 7
STRIDE = 8
UNITS = 3
DILATIONS = (1, 3, 9)
SPREAD = 3 * max(DILATIONS)
REACH = 3 * sum(DILATIONS)
ROWS = 16
EDGE = 48
LEAD = EDGE - STRIDE
SINE = (3.141592640130706, -5.167710083507895, 2.550077523214613, -0.5982912856202587, 0.07765766030474007)


def snake(values, frequency, inverse):
    turns = values * frequency
    rest = turns - jnp.round(turns)
    square = rest * rest
    poly = SINE[-1]
    for coefficient in SINE[-2::-1]:
        poly = poly * square + coefficient
    sine = poly * rest
    return values + sine * sine * inverse


def kernel(
    count, frames, tiles, chunks,
    up_hbm, taps_hbm, bias_wide_hbm, point_hbm, bias_point_hbm,
    alpha_in_hbm, beta_in_hbm, alpha_mid_hbm, beta_mid_hbm,
    out_ref,
    taps_ref, point_ref, ext_ref, x_ref, s_ref,
    bias_wide, bias_point, alpha_in, beta_in, alpha_mid, beta_mid,
    taps_sems, point_sems, small_sems, up_sem, send_sems, recv_sems,
):
    rows = tiles * ROWS
    extended = frames + 2 * EDGE
    me = lax.axis_index("tm")
    has_left = me > 0
    has_right = me < count - 1
    barrier = pltpu.get_barrier_semaphore()

    @pl.when(has_left)
    def _():
        pl.semaphore_signal(barrier, inc=1, device_id={"tm": me - 1}, device_id_type=MESH)

    @pl.when(has_right)
    def _():
        pl.semaphore_signal(barrier, inc=1, device_id={"tm": me + 1}, device_id_type=MESH)

    own = pltpu.make_async_copy(up_hbm, ext_ref.at[:, pl.ds(EDGE, frames), :], up_sem)
    own.start()
    smalls = [
        pltpu.make_async_copy(source, target, small_sems.at[i])
        for i, (source, target) in enumerate((
            (alpha_in_hbm, alpha_in), (beta_in_hbm, beta_in), (bias_wide_hbm, bias_wide),
            (alpha_mid_hbm, alpha_mid), (beta_mid_hbm, beta_mid), (bias_point_hbm, bias_point),
        ))
    ]
    for copy in smalls:
        copy.start()
    copies = [
        (
            pltpu.make_async_copy(taps_hbm.at[unit], taps_ref.at[unit], taps_sems.at[unit]),
            pltpu.make_async_copy(point_hbm.at[unit], point_ref.at[unit], point_sems.at[unit]),
        )
        for unit in range(UNITS)
    ]
    copies[0][0].start()

    @pl.when(has_left & has_right)
    def _():
        pl.semaphore_wait(barrier, 2)

    @pl.when(has_left != has_right)
    def _():
        pl.semaphore_wait(barrier, 1)

    to_right = pltpu.make_async_remote_copy(
        src_ref=up_hbm.at[:, pl.ds(frames - EDGE, EDGE), :],
        dst_ref=ext_ref.at[:, pl.ds(0, EDGE), :],
        send_sem=send_sems.at[0], recv_sem=recv_sems.at[0],
        device_id={"tm": me + 1}, device_id_type=MESH,
    )
    to_left = pltpu.make_async_remote_copy(
        src_ref=up_hbm.at[:, pl.ds(0, EDGE), :],
        dst_ref=ext_ref.at[:, pl.ds(EDGE + frames, EDGE), :],
        send_sem=send_sems.at[1], recv_sem=recv_sems.at[1],
        device_id={"tm": me - 1}, device_id_type=MESH,
    )

    @pl.when(has_right)
    def _():
        to_right.start()

    @pl.when(has_left)
    def _():
        to_left.start()

    for pair in copies:
        for copy in pair:
            if copy is not copies[0][0]:
                copy.start()

    @pl.when(jnp.logical_not(has_left))
    def _():
        ext_ref[:, 0:EDGE, :] = jnp.zeros((2, EDGE, ext_ref.shape[2]), jnp.bfloat16)

    @pl.when(jnp.logical_not(has_right))
    def _():
        ext_ref[:, EDGE + frames : extended, :] = jnp.zeros((2, EDGE, ext_ref.shape[2]), jnp.bfloat16)

    def frame_of(row):
        return (row & (ROWS - 1)) * tiles + (row >> 4)

    row = lax.broadcasted_iota(jnp.int32, (rows, 2 * extended), 0)
    column = lax.broadcasted_iota(jnp.int32, (rows, 2 * extended), 1)
    source = frame_of(row)
    hit = (column == source + STRIDE) | (column == source + extended)
    spread = jnp.where(hit, 1.0, 0.0).astype(jnp.bfloat16)
    for copy in smalls:
        copy.wait()
    own.wait()

    @pl.when(has_left)
    def _():
        to_right.wait_recv()

    @pl.when(has_right)
    def _():
        to_left.wait_recv()

    both = ext_ref[...].reshape(2 * extended, ext_ref.shape[2])
    x_ref[...] = jnp.dot(spread, both, preferred_element_type=jnp.float32).astype(jnp.bfloat16)

    lane_row = lax.broadcasted_iota(jnp.int32, (ROWS, 128), 0) * tiles
    first = LEAD - me * frames
    last = first + count * frames
    channels = x_ref.shape[1]

    for unit in range(UNITS):
        reach = 3 * DILATIONS[unit]
        frequency = alpha_in[unit : unit + 1, :] * (1.0 / math.pi)
        inverse = 1.0 / beta_in[unit : unit + 1, :]
        for tile in range(tiles):
            v = x_ref[tile * ROWS : (tile + 1) * ROWS, :].astype(jnp.float32)
            s = snake(v, frequency, inverse)
            where = lane_row + tile
            inside = (where >= first) & (where < last)
            s = jnp.concatenate(
                [jnp.where(inside, s[:, c : c + 128], 0.0) for c in range(0, channels, 128)], axis=1
            )
            start = (SPREAD + tile) * ROWS
            s_ref[start : start + ROWS, :] = s.astype(jnp.bfloat16)
            if tile >= tiles - reach:
                start = (SPREAD + tile - tiles) * ROWS
                s_ref[start : start + ROWS, :] = pltpu.roll(s, 1, 0).astype(jnp.bfloat16)
            if tile < reach:
                start = (SPREAD + tile + tiles) * ROWS
                s_ref[start : start + ROWS, :] = pltpu.roll(s, ROWS - 1, 0).astype(jnp.bfloat16)
        frequency = alpha_mid[unit : unit + 1, :] * (1.0 / math.pi)
        inverse = 1.0 / beta_mid[unit : unit + 1, :]
        copies[unit][0].wait()
        copies[unit][1].wait()
        begin = 0
        for size in chunks:
            length = size * ROWS
            stacked = jnp.concatenate(
                [
                    s_ref[pl.ds((SPREAD + begin + (k - 3) * DILATIONS[unit]) * ROWS, length), :]
                    for k in range(KERNEL)
                ],
                axis=1,
            )
            h = jnp.dot(stacked, taps_ref[unit], preferred_element_type=jnp.float32)
            h = h + bias_wide[unit : unit + 1, :]
            g = snake(h, frequency, inverse).astype(jnp.bfloat16)
            update = jnp.dot(g, point_ref[unit], preferred_element_type=jnp.float32)
            span = slice(begin * ROWS, begin * ROWS + length)
            kept = x_ref[span, :].astype(jnp.float32)
            x_ref[span, :] = (kept + (update + bias_point[unit : unit + 1, :])).astype(jnp.bfloat16)
            begin += size

    @pl.when(has_right)
    def _():
        to_right.wait_send()

    @pl.when(has_left)
    def _():
        to_left.wait_send()

    row = lax.broadcasted_iota(jnp.int32, (frames, rows), 0)
    column = lax.broadcasted_iota(jnp.int32, (frames, rows), 1)
    gather = jnp.where(frame_of(column) == row + LEAD, 1.0, 0.0).astype(jnp.bfloat16)
    out_ref[...] = jnp.dot(gather, x_ref[...], preferred_element_type=jnp.float32).astype(jnp.bfloat16)


def per_device(
    upsampled, taps, bias_wide, pointwise, bias_point, alpha_in, beta_in, alpha_mid, beta_mid
):
    count = lax.axis_size("tm")
    frames, channels = upsampled.shape[1:]
    tiles = -(-(frames + LEAD + REACH) // ROWS)
    rows = tiles * ROWS
    half = (tiles + 1) // 2
    vmem = pl.BlockSpec(memory_space=pltpu.VMEM)
    hbm = pl.BlockSpec(memory_space=pltpu.HBM)
    return pl.pallas_call(
        functools.partial(kernel, count, frames, tiles, (half, tiles - half)),
        out_shape=jax.ShapeDtypeStruct((frames, channels), jnp.bfloat16),
        in_specs=[hbm] * 9,
        out_specs=vmem,
        scratch_shapes=[
            pltpu.VMEM((UNITS, KERNEL * channels, channels), jnp.bfloat16),
            pltpu.VMEM((UNITS, channels, channels), jnp.bfloat16),
            pltpu.VMEM((2, frames + 2 * EDGE, channels), jnp.bfloat16),
            pltpu.VMEM((rows, channels), jnp.bfloat16),
            pltpu.VMEM((rows + 2 * SPREAD * ROWS, channels), jnp.bfloat16),
        ]
        + [pltpu.VMEM((UNITS, channels), jnp.float32)] * 6
        + [
            pltpu.SemaphoreType.DMA((UNITS,)),
            pltpu.SemaphoreType.DMA((UNITS,)),
            pltpu.SemaphoreType.DMA((6,)),
            pltpu.SemaphoreType.DMA,
            pltpu.SemaphoreType.DMA((2,)),
            pltpu.SemaphoreType.DMA((2,)),
        ],
        compiler_params=pltpu.CompilerParams(
            vmem_limit_bytes=63 << 20, collective_id=0, has_side_effects=True
        ),
    )(
        upsampled, taps.reshape(UNITS, KERNEL * channels, channels), bias_wide, pointwise,
        bias_point, alpha_in, beta_in, alpha_mid, beta_mid,
    )


def solution(mesh):
    placed = (P(None, ("grp", "tm"), None), P(), P(), P(), P(), P(), P(), P(), P())
    return jax.shard_map(
        per_device, mesh=mesh, in_specs=placed, out_specs=P(("grp", "tm"), None), check_vma=False
    )
```
